32 devices in a mesh: row: 2 (over core), col: 4 (over z), depth: 4 (over y, x).
Axes of the slice: x: 2, y: 2, z: 4, core: 2. Of those that a mesh axis runs over, the one named last changes fastest.
Arguments:
- tokens: bfloat16 [768, 4096], P(('col', 'depth'), 'row'), may hold values from -6 to 6
- cotangent: bfloat16 [768, 4096], P(('col', 'depth'), 'row'), may hold values from -6 to 6
- gate_weight: bfloat16 [4096, 14336], P(('row', 'depth'), 'col'), may hold values from -0.09375 to 0.09375
- up_weight: bfloat16 [4096, 14336], P(('row', 'depth'), 'col'), may hold values from -0.09375 to 0.09375
- down_weight: bfloat16 [14336, 4096], P('col', ('row', 'depth')), may hold values from -0.046875 to 0.046875
Outputs:
- output: bfloat16 [768, 4096], P(('col', 'depth'), 'row')
- input_grad: bfloat16 [768, 4096], P(('col', 'depth'), 'row')
- gate_grad: float32 [4096, 14336], P(('row', 'depth'), 'col')
- up_grad: float32 [4096, 14336], P(('row', 'depth'), 'col')
- down_grad: float32 [14336, 4096], P('col', ('row', 'depth'))
The draws below stay inside these ranges and needn't reach their ends.
All inputs are finite; a program needn't handle non-finite values.
Results may differ from the reference program's by a relative error of at most 0.0049.
Values may be sent and summed in bfloat16 or wider, within the bound.
No kernel may reach another device: no remote copies, remote signals or barrier semaphores. Data moves between devices by JAX's collectives and lax.ppermute only.
A program may use at most 192 MiB of HBM per device.

```python
import jax
import jax.numpy as jnp
from jax import lax

D = 4096
FF = 14336
TOKENS = 768


def block_levels(rng, dims, shards, smallest, largest):
    def one(position, blocks):
        heights = jax.random.uniform(jax.random.fold_in(jax.random.fold_in(rng, 6), position), (blocks,), jnp.float32, smallest / len(shards), largest / len(shards))
        return jnp.repeat(jnp.exp(heights), dims[position] // blocks).reshape((-1,) + (1,) * (len(dims) - position - 1))

    loudness = one(*shards[0])
    for cut in shards[1:]:
        loudness = loudness * one(*cut)
    return loudness


def normal_values(rng, extent, deviation, reach, pieces=(), dtype=jnp.bfloat16):
    result = deviation * jax.random.normal(rng, extent, jnp.float32)
    if pieces:
        result = result * block_levels(rng, extent, pieces, -0.22, 0.18)
    return jnp.clip(result, -reach, reach).astype(dtype)


def setup_inputs(seed: int = 0) -> dict:
    arg_keys = jax.random.split(jax.random.key(seed), 6)
    return {
        "tokens": normal_values(arg_keys[0], (TOKENS, D), 1.0, 6.0, ((0, 16), (1, 2))),
        "cotangent": normal_values(arg_keys[1], (TOKENS, D), 1.0, 6.0, ((0, 16), (1, 2))),
        "gate_weight": normal_values(arg_keys[2], (D, FF), D ** -0.5, 0.09375, ((0, 8), (1, 4))),
        "up_weight": normal_values(arg_keys[3], (D, FF), D ** -0.5, 0.09375, ((0, 8), (1, 4))),
        "down_weight": normal_values(arg_keys[4], (FF, D), FF ** -0.5, 0.046875, ((0, 4), (1, 8))),
    }


def dot_tn(left, right):
    return lax.dot_general(left, right, (((0,), (0,)), ((), ())), preferred_element_type=jnp.float32)


def dot_nt(left, right):
    return lax.dot_general(left, right, (((1,), (1,)), ((), ())), preferred_element_type=jnp.float32)


def reference(tokens, cotangent, gate_weight, up_weight, down_weight):
    gate = jnp.dot(tokens, gate_weight, preferred_element_type=jnp.float32)
    up = jnp.dot(tokens, up_weight, preferred_element_type=jnp.float32)
    sig = jax.nn.sigmoid(gate)
    hidden = (gate * sig * up).astype(jnp.bfloat16)
    output = jnp.dot(hidden, down_weight, preferred_element_type=jnp.float32).astype(jnp.bfloat16)
    hidden_grad = dot_nt(cotangent, down_weight)
    gate_delta = (hidden_grad * up * sig * (1.0 + gate * (1.0 - sig))).astype(jnp.bfloat16)
    up_delta = (hidden_grad * gate * sig).astype(jnp.bfloat16)
    input_grad = (dot_nt(gate_delta, gate_weight) + dot_nt(up_delta, up_weight)).astype(jnp.bfloat16)
    gate_grad = dot_tn(tokens, gate_delta)
    up_grad = dot_tn(tokens, up_delta)
    down_grad = dot_tn(hidden, cotangent)
    return output, input_grad, gate_grad, up_grad, down_grad
```

```python
import jax
import jax.numpy as jnp
from jax import lax
from jax.sharding import PartitionSpec as P

F32, BF16 = jnp.float32, jnp.bfloat16


def dot_nn(left, right):
    return jnp.dot(left, right, preferred_element_type=F32)


def dot_tn(left, right):
    return lax.dot_general(left, right, (((0,), (0,)), ((), ())), preferred_element_type=F32)


def dot_nt(left, right):
    return lax.dot_general(left, right, (((1,), (1,)), ((), ())), preferred_element_type=F32)


def deltas(hidden_grad, gate, up):
    sig = jax.nn.sigmoid(gate)
    gate_delta = (hidden_grad * up * sig * (1.0 + gate * (1.0 - sig))).astype(BF16)
    up_delta = (hidden_grad * gate * sig).astype(BF16)
    return gate_delta, up_delta


def activate(gate, up):
    return (gate * jax.nn.sigmoid(gate) * up).astype(BF16)


def make_on_device(mesh):
    n_row, n_col, n_depth = (mesh.shape[a] for a in ("row", "col", "depth"))
    assert n_depth == 4 and n_col % (2 * n_row) == 0

    def swap(x, axis, k):
        n = mesh.shape[axis]
        return lax.ppermute(x, axis, [(i, i ^ k) for i in range(n)])

    def on_device(tokens, cotangent, gate_weight, up_weight, down_weight):
        n, _ = tokens.shape
        feats = gate_weight.shape[0]
        r, d = lax.axis_index("row"), lax.axis_index("depth")
        js = n_col // n_row
        half = js // 2 * n

        gws = [gate_weight] + [swap(gate_weight, "row", i) for i in range(1, n_row)]
        uws = [up_weight] + [swap(up_weight, "row", i) for i in range(1, n_row)]
        dws = [down_weight] + [swap(down_weight, "row", i) for i in range(1, n_row)]

        def gather(x):
            blocks = []
            for k in range(n_depth):
                piece = lax.dynamic_slice(x, (0, (d ^ k) * feats), (n, feats))
                blocks.append(swap(piece, "depth", k) if k else piece)
            own = jnp.stack(blocks)
            cols = jnp.stack([own] + [swap(own, "col", j) for j in range(1, n_col)])
            cols = cols.reshape(n_row, 2, js // 2, n_depth, n, feats)
            cols = cols.transpose(0, 1, 3, 2, 4, 5).reshape(n_row, 2, n_depth, half, feats)
            order = [(0, 0), (1, 0), (0, 2), (1, 1), (0, 1), (0, 3), (1, 2), (1, 3)]
            return jnp.concatenate([cols[:, a, k] for a, k in order], axis=1)

        def spread(x):
            by_dist = [lax.dynamic_index_in_dim(x, r ^ i, 0, keepdims=False) for i in range(n_row)]
            shares = [by_dist[0]] + [swap(by_dist[i], "row", i) for i in range(1, n_row)]
            return shares, jnp.concatenate(by_dist, axis=0)

        tok_shares, tok_all = spread(gather(tokens))
        cot_shares, cot_all = spread(gather(cotangent))
        rows = half * 8

        def reduce_depth(shares, weights, dot):
            def part(lo, hi):
                total = dot(shares[0][lo:hi], weights[0])
                for s, w in zip(shares[1:], weights[1:]):
                    total = total + dot(s[lo:hi], w)
                return total

            sent = part(4 * half, 8 * half).astype(BF16)
            from_x = swap(sent[: 2 * half], "depth", 1)
            from_y = swap(sent[2 * half :], "depth", 2)
            keep = part(0, 4 * half)
            a2 = (keep[2 * half : 3 * half] + from_x[half:].astype(F32)).astype(BF16)
            b1 = (keep[3 * half :] + from_y[half:].astype(F32)).astype(BF16)
            last_y, last_x = swap(a2, "depth", 2), swap(b1, "depth", 1)
            a0 = keep[:half] + from_x[:half].astype(F32) + last_y.astype(F32)
            b0 = keep[half : 2 * half] + from_y[:half].astype(F32) + last_x.astype(F32)
            return jnp.concatenate([a0, b0], axis=0)

        def gather_depth(x):
            a0, b0 = x[:half], x[half:]
            a2, b1 = swap(a0, "depth", 2), swap(b0, "depth", 1)
            a13 = swap(jnp.concatenate([a0, a2]), "depth", 1)
            b23 = swap(jnp.concatenate([b0, b1]), "depth", 2)
            share = jnp.concatenate([x, a2, b1, a13, b23])
            return jnp.concatenate([share] + [swap(share, "row", i) for i in range(1, n_row)])

        def scatter(partial):
            by_dist = partial.reshape(n_row, rows, feats)
            mine = None
            for j in range(n_col):
                h, a, jj = j // js, (j % js) // (js // 2), j % (js // 2)
                share = lax.dynamic_index_in_dim(by_dist, r ^ h, 0, keepdims=False)
                share = share.reshape(8, js // 2, n, feats)[:, jj]
                picks = (0, 4, 2, 5) if a == 0 else (1, 3, 6, 7)
                piece = jnp.stack([share[p] for p in picks])
                piece = swap(piece, "col", j) if j else piece
                mine = piece if mine is None else mine + piece
            mine = mine.astype(BF16)
            out = jnp.zeros((n, feats * n_depth), BF16)
            for k in range(n_depth):
                piece = swap(mine[k], "depth", k) if k else mine[k]
                out = lax.dynamic_update_slice(out, piece, (0, (d ^ k) * feats))
            return out

        gate = reduce_depth(tok_shares, gws, dot_nn)
        up = reduce_depth(tok_shares, uws, dot_nn)
        hid_all = gather_depth(activate(gate, up))
        hidden_grad = reduce_depth(cot_shares, dws, dot_nt)
        gate_delta, up_delta = deltas(hidden_grad, gate, up)
        output = scatter(dot_nn(hid_all, down_weight))
        gd_all, ud_all = gather_depth(gate_delta), gather_depth(up_delta)
        down_grad = dot_tn(hid_all, cot_all)
        gate_grad = dot_tn(tok_all, gd_all)
        input_grad = scatter(dot_nt(gd_all, gate_weight) + dot_nt(ud_all, up_weight))
        up_grad = dot_tn(tok_all, ud_all)
        return output, input_grad, gate_grad, up_grad, down_grad

    return on_device


def solution(mesh):
    act = P(("col", "depth"), "row")
    wide = P(("row", "depth"), "col")
    tall = P("col", ("row", "depth"))
    return jax.shard_map(
        make_on_device(mesh),
        mesh=mesh,
        in_specs=(act, act, wide, wide, tall),
        out_specs=(act, act, wide, wide, tall),
        check_vma=False,
    )
```

```python
import jax
import jax.numpy as jnp
from jax import lax
from jax.sharding import PartitionSpec as P

F32, BF16 = jnp.float32, jnp.bfloat16


def dot_nn(left, right):
    return jnp.dot(left, right, preferred_element_type=F32)


def dot_tn(left, right):
    return lax.dot_general(left, right, (((0,), (0,)), ((), ())), preferred_element_type=F32)


def dot_nt(left, right):
    return lax.dot_general(left, right, (((1,), (1,)), ((), ())), preferred_element_type=F32)


def deltas(hidden_grad, gate, up):
    sig = jax.nn.sigmoid(gate)
    gate_delta = (hidden_grad * up * sig * (1.0 + gate * (1.0 - sig))).astype(BF16)
    up_delta = (hidden_grad * gate * sig).astype(BF16)
    return gate_delta, up_delta


def activate(gate, up):
    return (gate * jax.nn.sigmoid(gate) * up).astype(BF16)


def make_on_device(mesh):
    n_row, n_col, n_depth = (mesh.shape[a] for a in ("row", "col", "depth"))
    assert n_depth == 4 and n_col == 2 * n_row
    order = [(0, 0), (1, 0), (0, 2), (1, 1), (0, 1), (0, 3), (1, 2), (1, 3)]
    barrier = lax.optimization_barrier

    def swap(x, axis, k):
        n = mesh.shape[axis]
        return lax.ppermute(x, axis, [(i, i ^ k) for i in range(n)])

    def on_device(tokens, cotangent, gate_weight, up_weight, down_weight):
        n, _ = tokens.shape
        feats = gate_weight.shape[0]
        r, d = lax.axis_index("row"), lax.axis_index("depth")

        def by_row(x):
            return [lax.dynamic_index_in_dim(x, r ^ i, 0, keepdims=False) for i in range(n_row)]

        both = jnp.stack([tokens, cotangent])
        own = [lax.dynamic_slice(both, (0, 0, (d ^ k) * feats), (2, n, feats)) for k in range(n_depth)]
        own = jnp.stack([swap(x, "depth", k) if k else x for k, x in enumerate(own)], axis=1)

        def more_cols(cols, k):
            got = swap(jnp.stack(list(cols.values())), "col", k)
            return {**cols, **{j ^ k: got[i] for i, j in enumerate(cols)}}

        def all_cols(cols, k):
            while k:
                cols = more_cols(cols, k)
                k //= 2
            shares = [jnp.concatenate([cols[2 * h + a][k] for a, k in order]) for h in range(n_row)]
            return by_row(jnp.stack(shares))

        def spread(shares):
            return [shares[0]] + [swap(shares[i], "row", i) for i in range(1, n_row)]

        def tiles(w):
            return [w] + [swap(w, "row", i) for i in range(1, n_row)]

        def part(shares, weights, dot, lo, hi):
            total = dot(shares[0][lo:hi], weights[0])
            for s, w in zip(shares[1:], weights[1:]):
                total = total + dot(s[lo:hi], w)
            return total

        def send_first(sent):
            return swap(sent[: 2 * n], "depth", 1), swap(sent[2 * n :], "depth", 2)

        def second(keep, from_x, from_y):
            a2 = (keep[2 * n : 3 * n] + from_x[n:].astype(F32)).astype(BF16)
            b1 = (keep[3 * n :] + from_y[n:].astype(F32)).astype(BF16)
            return a2, b1

        def total(keep, from_x, from_y, last_y, last_x):
            a0 = keep[:n] + from_x[:n].astype(F32) + last_y.astype(F32)
            b0 = keep[n : 2 * n] + from_y[:n].astype(F32) + last_x.astype(F32)
            return a0, b0

        def gather_row(*blocks):
            x = jnp.concatenate(blocks)
            return [x] + [swap(x, "row", i) for i in range(1, n_row)]

        def cross(b_blocks):
            return swap(b_blocks.astype(BF16), "col", 1).astype(F32)

        def finish(x):
            xs, k = dict(enumerate(by_row(x))), 1
            while k < n_row:
                hs = [h for h in xs if h & k]
                got = swap(jnp.stack([xs.pop(h) for h in hs]).astype(BF16), "col", 2 * k).astype(F32)
                for i, h in enumerate(hs):
                    xs[h ^ k] = xs[h ^ k] + got[i]
                k *= 2
            return xs[0].astype(BF16)

        def place(*sums):
            outs = jnp.zeros((len(sums), n, feats * n_depth), BF16)
            for k in range(n_depth):
                piece = jnp.stack([x[k] for x in sums])
                piece = swap(piece, "depth", k) if k else piece
                outs = lax.dynamic_update_slice(outs, piece, (0, 0, (d ^ k) * feats))
            return [outs[i] for i in range(len(sums))]

        gws, uws, dws = tiles(gate_weight), tiles(up_weight), tiles(down_weight)
        tok = all_cols({0: own[0]}, n_col // 2)
        cot_own, tok = barrier((own[1], tok))
        tok_shares = spread(tok)
        tok_all = jnp.concatenate(tok).T

        gate_sent = part(tok_shares, gws, dot_nn, 4 * n, 8 * n).astype(BF16)
        gate_got = send_first(gate_sent)
        cot_cols = more_cols({0: cot_own}, n_col // 2)
        tok_shares, gate_sent = barrier((tok_shares, gate_sent))
        up_sent = part(tok_shares, uws, dot_nn, 4 * n, 8 * n).astype(BF16)
        up_got = send_first(up_sent)
        tok_shares, cot_cols, gate_got, up_sent = barrier((tok_shares, cot_cols, gate_got, up_sent))
        cot = all_cols(cot_cols, n_col // 4)
        gate_keep = part(tok_shares, gws, dot_nn, 0, 4 * n)
        a2, b1 = second(gate_keep, *gate_got)
        gate_last = swap(a2, "depth", 2), swap(b1, "depth", 1)
        tok_shares, cot, a2, b1 = barrier((tok_shares, cot, a2, b1))
        up_keep = part(tok_shares, uws, dot_nn, 0, 4 * n)
        cot_shares = spread(cot)
        back_sent = part(cot_shares, dws, dot_nt, 4 * n, 8 * n).astype(BF16)
        back_got = send_first(back_sent)
        up_got, cot_shares, back_sent = barrier((up_got, cot_shares, back_sent))
        a2, b1 = second(up_keep, *up_got)
        up_last = swap(a2, "depth", 2), swap(b1, "depth", 1)
        cot_shares, a2, b1 = barrier((cot_shares, a2, b1))
        back_keep = part(cot_shares, dws, dot_nt, 0, 4 * n)

        gate = total(gate_keep, *gate_got, *gate_last)
        up = total(up_keep, *up_got, *up_last)
        h_a0, h_b0 = [activate(g, u) for g, u in zip(gate, up)]
        h_a2, h_b1 = swap(h_a0, "depth", 2), swap(h_b0, "depth", 1)
        back_got, h_a0, h_b0 = barrier((back_got, h_a0, h_b0))
        a2, b1 = second(back_keep, *back_got)
        back_last = swap(a2, "depth", 2), swap(b1, "depth", 1)
        h_a2, h_b1, a2, b1 = barrier((h_a2, h_b1, a2, b1))
        h_from_x = swap(jnp.concatenate([h_a0, h_a2]), "depth", 1)
        h_from_y = swap(jnp.concatenate([h_b0, h_b1]), "depth", 2)
        hidden_grad = total(back_keep, *back_got, *back_last)
        d_a0, d_b0 = [jnp.concatenate(deltas(h, g, u)) for h, g, u in zip(hidden_grad, gate, up)]
        d_a2, d_b1 = swap(d_a0, "depth", 2), swap(d_b0, "depth", 1)

        def back(rows):
            blocks = rows[0].shape[0] // (2 * n)
            rows = [x.reshape(blocks, 2, n, -1) for x in rows]
            gd, ud = [[x[:, i].reshape(blocks * n, -1) for x in rows] for i in range(2)]
            sums = [dot_nt(g, gate_weight) + dot_nt(u, up_weight) for g, u in zip(gd, ud)]
            return gd, ud, jnp.stack(sums).reshape(n_row, blocks, n, feats)

        gd_e, ud_e, early = back(gather_row(d_a0, d_b0))
        h_from_x, h_from_y, early = barrier((h_from_x, h_from_y, early))
        hid_rows = gather_row(h_a0, h_b0, h_a2, h_b1, h_from_x, h_from_y)
        out = jnp.stack([dot_nn(x, down_weight) for x in hid_rows]).reshape(n_row, 8, n, feats)
        got = cross(jnp.concatenate([jnp.stack([out[:, i] for i in (1, 3, 6, 7)], axis=1), early[:, 1:]], axis=1))
        hid_rows, cot, out = barrier((hid_rows, cot, out))
        down_grad = dot_tn(jnp.concatenate(hid_rows), jnp.concatenate(cot))

        d_a2, d_b1, down_grad = barrier((d_a2, d_b1, down_grad))
        from_x = swap(jnp.concatenate([d_a0, d_a2]), "depth", 1)
        from_y = swap(jnp.concatenate([d_b0, d_b1]), "depth", 2)
        middle = gather_row(d_a2, d_b1)
        z_out = jnp.stack([out[:, i] for i in (0, 4, 2, 5)], axis=1) + got[:, :4]
        done = finish(jnp.concatenate([z_out, early[:, :1] + got[:, 4:]], axis=1))
        from_x, from_y, middle, done = barrier((from_x, from_y, middle, done))
        late = [jnp.concatenate(x) for x in zip(middle, gather_row(from_x, from_y))]
        gd_l, ud_l, late = back(late)
        tok_all, late = barrier((tok_all, late))
        got_l = cross(jnp.stack([late[:, i] for i in (1, 4, 5)], axis=1))

        def by_share(e, l):
            return jnp.concatenate([x for pair in zip(e, l) for x in pair])

        gate_grad = dot_nn(tok_all, by_share(gd_e, gd_l))
        tok_all, got_l, gate_grad = barrier((tok_all, got_l, gate_grad))
        rest = finish(jnp.stack([late[:, i] for i in (2, 0, 3)], axis=1) + got_l)
        output, input_grad = place(done[:4], [done[4], *rest])
        up_grad = dot_nn(tok_all, by_share(ud_e, ud_l))
        return output, input_grad, gate_grad, up_grad, down_grad

    return on_device


def solution(mesh):
    act = P(("col", "depth"), "row")
    wide = P(("row", "depth"), "col")
    tall = P("col", ("row", "depth"))
    return jax.shard_map(
        make_on_device(mesh),
        mesh=mesh,
        in_specs=(act, act, wide, wide, tall),
        out_specs=(act, act, wide, wide, tall),
        check_vma=False,
    )
```

```python
import jax
import jax.numpy as jnp
from jax import lax
from jax.sharding import PartitionSpec as P

F32, BF16 = jnp.float32, jnp.bfloat16


def dot_nn(left, right):
    return jnp.dot(left, right, preferred_element_type=F32)


def dot_tn(left, right):
    return lax.dot_general(left, right, (((0,), (0,)), ((), ())), preferred_element_type=F32)


def dot_nt(left, right):
    return lax.dot_general(left, right, (((1,), (1,)), ((), ())), preferred_element_type=F32)


def deltas(hidden_grad, gate, up):
    sig = jax.nn.sigmoid(gate)
    gate_delta = (hidden_grad * up * sig * (1.0 + gate * (1.0 - sig))).astype(BF16)
    up_delta = (hidden_grad * gate * sig).astype(BF16)
    return gate_delta, up_delta


def activate(gate, up):
    return (gate * jax.nn.sigmoid(gate) * up).astype(BF16)


def make_on_device(mesh):
    n_row, n_col, n_depth = (mesh.shape[a] for a in ("row", "col", "depth"))
    assert n_depth == 4 and n_col == 2 * n_row
    order = [(0, 0), (1, 0), (0, 2), (1, 1), (0, 1), (0, 3), (1, 2), (1, 3)]
    barrier = lax.optimization_barrier

    def swap(x, axis, k):
        n = mesh.shape[axis]
        return lax.ppermute(x, axis, [(i, i ^ k) for i in range(n)])

    def on_device(tokens, cotangent, gate_weight, up_weight, down_weight):
        n, _ = tokens.shape
        feats = gate_weight.shape[0]
        r, d = lax.axis_index("row"), lax.axis_index("depth")

        def by_row(x):
            return [lax.dynamic_index_in_dim(x, r ^ i, 0, keepdims=False) for i in range(n_row)]

        def gather_feats(x):
            pieces = [lax.dynamic_slice(x, (0, 0, (d ^ k) * feats), (2, n, feats)) for k in range(n_depth)]
            pieces = [swap(x, "depth", k) if k else x for k, x in enumerate(pieces)]
            return [[x[i] for x in pieces] for i in range(2)]

        def more_cols(cols, k):
            got = swap(jnp.stack(list(cols.values())), "col", k)
            return {**cols, **{j ^ k: got[i] for i, j in enumerate(cols)}}

        def all_cols(cols, k):
            while k:
                cols = more_cols(cols, k)
                k //= 2
            return cols

        def shares(*parts):
            by_h = [
                jnp.concatenate([parts[k // 2][2 * h + a][k % 2] for a, k in order]) for h in range(n_row)
            ]
            return by_row(jnp.stack(by_h))

        def spread(shares):
            return [shares[0]] + [swap(shares[i], "row", i) for i in range(1, n_row)]

        def tiles(w):
            return [w] + [swap(w, "row", i) for i in range(1, n_row)]

        def part(shares, weights, dot, lo, hi):
            total = dot(shares[0][lo:hi], weights[0])
            for s, w in zip(shares[1:], weights[1:]):
                total = total + dot(s[lo:hi], w)
            return total

        def send_first(sent):
            return swap(sent[: 2 * n], "depth", 1), swap(sent[2 * n :], "depth", 2)

        def second(keep, from_x, from_y):
            a2 = (keep[2 * n : 3 * n] + from_x[n:].astype(F32)).astype(BF16)
            b1 = (keep[3 * n :] + from_y[n:].astype(F32)).astype(BF16)
            return a2, b1

        def total(keep, from_x, from_y, last_y, last_x):
            a0 = keep[:n] + from_x[:n].astype(F32) + last_y.astype(F32)
            b0 = keep[n : 2 * n] + from_y[:n].astype(F32) + last_x.astype(F32)
            return a0, b0

        def gather_row(*blocks):
            x = jnp.concatenate(blocks)
            return [x] + [swap(x, "row", i) for i in range(1, n_row)]

        def cross(b_blocks):
            return swap(b_blocks.astype(BF16), "col", 1).astype(F32)

        def finish(x):
            xs, k = dict(enumerate(by_row(x))), 1
            while k < n_row:
                hs = [h for h in xs if h & k]
                got = swap(jnp.stack([xs.pop(h) for h in hs]).astype(BF16), "col", 2 * k).astype(F32)
                for i, h in enumerate(hs):
                    xs[h ^ k] = xs[h ^ k] + got[i]
                k *= 2
            return xs[0].astype(BF16)

        def direct(a_blocks, b_blocks):
            xs = [x for pair in zip(by_row(a_blocks), by_row(b_blocks)) for x in pair]
            got = [swap(x.astype(BF16), "col", j).astype(F32) for j, x in enumerate(xs) if j]
            return sum(got, xs[0]).astype(BF16)

        def place(*sums):
            outs = jnp.zeros((len(sums), n, feats * n_depth), BF16)
            for k in range(n_depth):
                piece = jnp.stack([x[k] for x in sums])
                piece = swap(piece, "depth", k) if k else piece
                outs = lax.dynamic_update_slice(outs, piece, (0, 0, (d ^ k) * feats))
            return [outs[i] for i in range(len(sums))]

        gws, uws, dws = tiles(gate_weight), tiles(up_weight), tiles(down_weight)
        far, near = n_col // 2, n_col // 4
        tok_own, cot_own = gather_feats(jnp.stack([tokens, cotangent]))
        tok_1, tok_2 = [more_cols({0: jnp.stack(tok_own[i : i + 2])}, far) for i in (0, 2)]
        tok = shares(all_cols(tok_1, near), all_cols(tok_2, near))
        cot_own = jnp.stack(cot_own)
        cot_own, tok = barrier((cot_own, tok))
        tok_shares = spread(tok)
        tok_all = jnp.concatenate(tok).T

        gate_sent = part(tok_shares, gws, dot_nn, 4 * n, 8 * n).astype(BF16)
        gate_got = send_first(gate_sent)
        cot_cols = more_cols({0: cot_own}, far)
        tok_shares, gate_sent = barrier((tok_shares, gate_sent))
        up_sent = part(tok_shares, uws, dot_nn, 4 * n, 8 * n).astype(BF16)
        up_got = send_first(up_sent)
        tok_shares, cot_cols, gate_got, up_sent = barrier((tok_shares, cot_cols, gate_got, up_sent))
        cot_cols = all_cols(cot_cols, near)
        cot = shares({j: x[:2] for j, x in cot_cols.items()}, {j: x[2:] for j, x in cot_cols.items()})
        gate_keep = part(tok_shares, gws, dot_nn, 0, 4 * n)
        a2, b1 = second(gate_keep, *gate_got)
        gate_last = swap(a2, "depth", 2), swap(b1, "depth", 1)
        tok_shares, cot, a2, b1 = barrier((tok_shares, cot, a2, b1))
        up_keep = part(tok_shares, uws, dot_nn, 0, 4 * n)
        cot_shares = spread(cot)
        back_sent = part(cot_shares, dws, dot_nt, 4 * n, 8 * n).astype(BF16)
        back_got = send_first(back_sent)
        up_got, cot_shares, back_sent = barrier((up_got, cot_shares, back_sent))
        a2, b1 = second(up_keep, *up_got)
        up_last = swap(a2, "depth", 2), swap(b1, "depth", 1)
        cot_shares, a2, b1 = barrier((cot_shares, a2, b1))
        back_keep = part(cot_shares, dws, dot_nt, 0, 4 * n)

        gate = total(gate_keep, *gate_got, *gate_last)
        up = total(up_keep, *up_got, *up_last)
        h_a0, h_b0 = [activate(g, u) for g, u in zip(gate, up)]
        h_a2, h_b1 = swap(h_a0, "depth", 2), swap(h_b0, "depth", 1)
        back_got, h_a0, h_b0 = barrier((back_got, h_a0, h_b0))
        a2, b1 = second(back_keep, *back_got)
        back_last = swap(a2, "depth", 2), swap(b1, "depth", 1)
        h_a2, h_b1, a2, b1 = barrier((h_a2, h_b1, a2, b1))
        h_from_x = swap(jnp.concatenate([h_a0, h_a2]), "depth", 1)
        h_from_y = swap(jnp.concatenate([h_b0, h_b1]), "depth", 2)
        hidden_grad = total(back_keep, *back_got, *back_last)
        d_a0, d_b0 = [jnp.concatenate(deltas(h, g, u)) for h, g, u in zip(hidden_grad, gate, up)]
        d_a2, d_b1 = swap(d_a0, "depth", 2), swap(d_b0, "depth", 1)

        def back(rows):
            blocks = rows[0].shape[0] // (2 * n)
            rows = [x.reshape(blocks, 2, n, -1) for x in rows]
            gd, ud = [[x[:, i].reshape(blocks * n, -1) for x in rows] for i in range(2)]
            sums = [dot_nt(g, gate_weight) + dot_nt(u, up_weight) for g, u in zip(gd, ud)]
            return gd, ud, jnp.stack(sums).reshape(n_row, blocks, n, feats)

        gd_e, ud_e, early = back(gather_row(d_a0, d_b0))
        h_from_x, h_from_y, early = barrier((h_from_x, h_from_y, early))
        hid_rows = gather_row(h_a0, h_b0, h_a2, h_b1, h_from_x, h_from_y)
        out = jnp.stack([dot_nn(x, down_weight) for x in hid_rows]).reshape(n_row, 8, n, feats)
        d_a2, d_b1, out = barrier((d_a2, d_b1, out))
        from_x = swap(jnp.concatenate([d_a0, d_a2]), "depth", 1)
        from_y = swap(jnp.concatenate([d_b0, d_b1]), "depth", 2)
        middle = gather_row(d_a2, d_b1)
        hid_rows, cot, out, middle = barrier((hid_rows, cot, out, middle))
        done = direct(
            jnp.concatenate([jnp.stack([out[:, i] for i in (0, 4, 2, 5)], axis=1), early[:, :1]], axis=1),
            jnp.concatenate([jnp.stack([out[:, i] for i in (1, 3, 6, 7)], axis=1), early[:, 1:]], axis=1),
        )
        down_grad = dot_tn(jnp.concatenate(hid_rows), jnp.concatenate(cot))
        from_x, from_y, middle, done = barrier((from_x, from_y, middle, done))
        late = [jnp.concatenate(x) for x in zip(middle, gather_row(from_x, from_y))]
        gd_l, ud_l, late = back(late)
        tok_all, late = barrier((tok_all, late))
        got_l = cross(jnp.stack([late[:, i] for i in (1, 4, 5)], axis=1))

        def by_share(e, l):
            return jnp.concatenate([x for pair in zip(e, l) for x in pair])

        gate_grad = dot_nn(tok_all, by_share(gd_e, gd_l))
        tok_all, got_l, gate_grad = barrier((tok_all, got_l, gate_grad))
        rest = finish(jnp.stack([late[:, i] for i in (2, 0, 3)], axis=1) + got_l)
        output, input_grad = place(done[:4], [done[4], *rest])
        up_grad = dot_nn(tok_all, by_share(ud_e, ud_l))
        return output, input_grad, gate_grad, up_grad, down_grad

    return on_device


def solution(mesh):
    act = P(("col", "depth"), "row")
    wide = P(("row", "depth"), "col")
    tall = P("col", ("row", "depth"))
    return jax.shard_map(
        make_on_device(mesh),
        mesh=mesh,
        in_specs=(act, act, wide, wide, tall),
        out_specs=(act, act, wide, wide, tall),
        check_vma=False,
    )
```

```python
import jax
import jax.numpy as jnp
from jax import lax
from jax.sharding import PartitionSpec as P

F32, BF16 = jnp.float32, jnp.bfloat16


def dot_nn(left, right):
    return jnp.dot(left, right, preferred_element_type=F32)


def dot_tn(left, right):
    return lax.dot_general(left, right, (((0,), (0,)), ((), ())), preferred_element_type=F32)


def dot_nt(left, right):
    return lax.dot_general(left, right, (((1,), (1,)), ((), ())), preferred_element_type=F32)


def deltas(hidden_grad, gate, up):
    sig = jax.nn.sigmoid(gate)
    gate_delta = (hidden_grad * up * sig * (1.0 + gate * (1.0 - sig))).astype(BF16)
    up_delta = (hidden_grad * gate * sig).astype(BF16)
    return gate_delta, up_delta


def activate(gate, up):
    return (gate * jax.nn.sigmoid(gate) * up).astype(BF16)


def make_on_device(mesh):
    n_row, n_col, n_depth = (mesh.shape[a] for a in ("row", "col", "depth"))
    assert n_depth == 4 and n_col == 2 * n_row
    order = [(0, 0), (1, 0), (0, 2), (1, 1), (0, 1), (0, 3), (1, 2), (1, 3)]
    barrier = lax.optimization_barrier

    def swap(x, axis, k):
        n = mesh.shape[axis]
        return lax.ppermute(x, axis, [(i, i ^ k) for i in range(n)])

    def on_device(tokens, cotangent, gate_weight, up_weight, down_weight):
        n, _ = tokens.shape
        feats = gate_weight.shape[0]
        r, d = lax.axis_index("row"), lax.axis_index("depth")

        def by_row(x):
            return [lax.dynamic_index_in_dim(x, r ^ i, 0, keepdims=False) for i in range(n_row)]

        def gather_feats(x):
            pieces = [lax.dynamic_slice(x, (0, 0, (d ^ k) * feats), (2, n, feats)) for k in range(n_depth)]
            pieces = [swap(x, "depth", k) if k else x for k, x in enumerate(pieces)]
            return [[x[i] for x in pieces] for i in range(2)]

        def more_cols(cols, k):
            got = swap(jnp.stack(list(cols.values())), "col", k)
            return {**cols, **{j ^ k: got[i] for i, j in enumerate(cols)}}

        def all_cols(cols, k):
            while k:
                cols = more_cols(cols, k)
                k //= 2
            return cols

        def shares(*parts):
            by_h = [
                jnp.concatenate([parts[k // 2][2 * h + a][k % 2] for a, k in order]) for h in range(n_row)
            ]
            return by_row(jnp.stack(by_h))

        def spread(shares):
            return [shares[0]] + [swap(shares[i], "row", i) for i in range(1, n_row)]

        def tiles(w):
            return [w] + [swap(w, "row", i) for i in range(1, n_row)]

        def part(shares, weights, dot, lo, hi):
            total = dot(shares[0][lo:hi], weights[0])
            for s, w in zip(shares[1:], weights[1:]):
                total = total + dot(s[lo:hi], w)
            return total

        def send_first(sent):
            return swap(sent[: 2 * n], "depth", 1), swap(sent[2 * n :], "depth", 2)

        def second(keep, from_x, from_y):
            a2 = (keep[2 * n : 3 * n] + from_x[n:].astype(F32)).astype(BF16)
            b1 = (keep[3 * n :] + from_y[n:].astype(F32)).astype(BF16)
            return a2, b1

        def total(keep, from_x, from_y, last_y, last_x):
            a0 = keep[:n] + from_x[:n].astype(F32) + last_y.astype(F32)
            b0 = keep[n : 2 * n] + from_y[:n].astype(F32) + last_x.astype(F32)
            return a0, b0

        def gather_row(*blocks):
            x = jnp.concatenate(blocks)
            return [x] + [swap(x, "row", i) for i in range(1, n_row)]

        def cross(b_blocks):
            return swap(b_blocks.astype(BF16), "col", 1).astype(F32)

        def finish(x):
            xs, k = dict(enumerate(by_row(x))), 1
            while k < n_row:
                hs = [h for h in xs if h & k]
                got = swap(jnp.stack([xs.pop(h) for h in hs]).astype(BF16), "col", 2 * k).astype(F32)
                for i, h in enumerate(hs):
                    xs[h ^ k] = xs[h ^ k] + got[i]
                k *= 2
            return xs[0].astype(BF16)

        def direct(a_blocks, b_blocks):
            xs = [x for pair in zip(by_row(a_blocks), by_row(b_blocks)) for x in pair]
            got = [swap(x.astype(BF16), "col", j).astype(F32) for j, x in enumerate(xs) if j]
            return sum(got, xs[0]).astype(BF16)

        def place(*sums):
            outs = jnp.zeros((len(sums), n, feats * n_depth), BF16)
            for k in range(n_depth):
                piece = jnp.stack([x[k] for x in sums])
                piece = swap(piece, "depth", k) if k else piece
                outs = lax.dynamic_update_slice(outs, piece, (0, 0, (d ^ k) * feats))
            return [outs[i] for i in range(len(sums))]

        gws, uws, dws = tiles(gate_weight), tiles(up_weight), tiles(down_weight)
        far, near = n_col // 2, n_col // 4
        tok_own, cot_own = gather_feats(jnp.stack([tokens, cotangent]))
        tok_1, tok_2 = [more_cols({0: jnp.stack(tok_own[i : i + 2])}, far) for i in (0, 2)]
        cot_own, tok_1 = barrier((jnp.stack(cot_own), all_cols(tok_1, near)))
        tok = shares(tok_1, all_cols(tok_2, near))
        tok_shares = spread(tok)
        tok_all = jnp.concatenate(tok).T

        gate_sent = part(tok_shares, gws, dot_nn, 4 * n, 8 * n).astype(BF16)
        gate_got = send_first(gate_sent)
        cot_cols = more_cols({0: cot_own}, far)
        tok_shares, gate_sent = barrier((tok_shares, gate_sent))
        up_sent = part(tok_shares, uws, dot_nn, 4 * n, 8 * n).astype(BF16)
        up_got = send_first(up_sent)
        tok_shares, cot_cols, gate_got, up_sent = barrier((tok_shares, cot_cols, gate_got, up_sent))
        cot_cols = all_cols(cot_cols, near)
        cot = shares({j: x[:2] for j, x in cot_cols.items()}, {j: x[2:] for j, x in cot_cols.items()})
        gate_keep = part(tok_shares, gws, dot_nn, 0, 4 * n)
        a2, b1 = second(gate_keep, *gate_got)
        gate_last = swap(a2, "depth", 2), swap(b1, "depth", 1)
        tok_shares, cot, a2, b1 = barrier((tok_shares, cot, a2, b1))
        up_keep = part(tok_shares, uws, dot_nn, 0, 4 * n)
        cot_shares = spread(cot)
        back_sent = part(cot_shares, dws, dot_nt, 4 * n, 8 * n).astype(BF16)
        back_got = send_first(back_sent)
        up_got, cot_shares, back_sent = barrier((up_got, cot_shares, back_sent))
        a2, b1 = second(up_keep, *up_got)
        up_last = swap(a2, "depth", 2), swap(b1, "depth", 1)
        cot_shares, a2, b1 = barrier((cot_shares, a2, b1))
        back_keep = part(cot_shares, dws, dot_nt, 0, 4 * n)

        gate = total(gate_keep, *gate_got, *gate_last)
        up = total(up_keep, *up_got, *up_last)
        h_a0, h_b0 = [activate(g, u) for g, u in zip(gate, up)]
        h_a2, h_b1 = swap(h_a0, "depth", 2), swap(h_b0, "depth", 1)
        back_got, h_a0, h_b0 = barrier((back_got, h_a0, h_b0))
        a2, b1 = second(back_keep, *back_got)
        back_last = swap(a2, "depth", 2), swap(b1, "depth", 1)
        h_a2, h_b1, a2, b1 = barrier((h_a2, h_b1, a2, b1))
        h_from_x = swap(jnp.concatenate([h_a0, h_a2]), "depth", 1)
        h_from_y = swap(jnp.concatenate([h_b0, h_b1]), "depth", 2)
        hidden_grad = total(back_keep, *back_got, *back_last)
        d_a0, d_b0 = [jnp.concatenate(deltas(h, g, u)) for h, g, u in zip(hidden_grad, gate, up)]
        d_a2, d_b1 = swap(d_a0, "depth", 2), swap(d_b0, "depth", 1)

        def back(rows):
            blocks = rows[0].shape[0] // (2 * n)
            rows = [x.reshape(blocks, 2, n, -1) for x in rows]
            gd, ud = [[x[:, i].reshape(blocks * n, -1) for x in rows] for i in range(2)]
            sums = [dot_nt(g, gate_weight) + dot_nt(u, up_weight) for g, u in zip(gd, ud)]
            return gd, ud, jnp.stack(sums).reshape(n_row, blocks, n, feats)

        gd_e, ud_e, early = back(gather_row(d_a0, d_b0))
        h_from_x, h_from_y, d_a2, d_b1, early = barrier((h_from_x, h_from_y, d_a2, d_b1, early))
        from_x = swap(jnp.concatenate([d_a0, d_a2]), "depth", 1)
        from_y = swap(jnp.concatenate([d_b0, d_b1]), "depth", 2)
        hid_rows = gather_row(h_a0, h_b0, h_a2, h_b1, h_from_x, h_from_y)
        out = jnp.stack([dot_nn(x, down_weight) for x in hid_rows]).reshape(n_row, 8, n, feats)
        middle = gather_row(d_a2, d_b1)
        hid_rows, cot, out = barrier((hid_rows, cot, out))
        done = direct(
            jnp.concatenate([jnp.stack([out[:, i] for i in (0, 4, 2, 5)], axis=1), early[:, :1]], axis=1),
            jnp.concatenate([jnp.stack([out[:, i] for i in (1, 3, 6, 7)], axis=1), early[:, 1:]], axis=1),
        )
        down_grad = dot_tn(jnp.concatenate(hid_rows), jnp.concatenate(cot))
        from_x, from_y, middle, done = barrier((from_x, from_y, middle, done))
        late = [jnp.concatenate(x) for x in zip(middle, gather_row(from_x, from_y))]
        gd_l, ud_l, late = back(late)
        tok_all, late = barrier((tok_all, late))
        got_l = cross(jnp.stack([late[:, i] for i in (1, 4, 5)], axis=1))

        def by_share(e, l):
            return jnp.concatenate([x for pair in zip(e, l) for x in pair])

        gate_grad = dot_nn(tok_all, by_share(gd_e, gd_l))
        tok_all, got_l, gate_grad = barrier((tok_all, got_l, gate_grad))
        rest = finish(jnp.stack([late[:, i] for i in (2, 0, 3)], axis=1) + got_l)
        output, input_grad = place(done[:4], [done[4], *rest])
        up_grad = dot_nn(tok_all, by_share(ud_e, ud_l))
        return output, input_grad, gate_grad, up_grad, down_grad

    return on_device


def solution(mesh):
    act = P(("col", "depth"), "row")
    wide = P(("row", "depth"), "col")
    tall = P("col", ("row", "depth"))
    return jax.shard_map(
        make_on_device(mesh),
        mesh=mesh,
        in_specs=(act, act, wide, wide, tall),
        out_specs=(act, act, wide, wide, tall),
        check_vma=False,
    )
```

```python
import jax
import jax.numpy as jnp
from jax import lax
from jax.sharding import PartitionSpec as P

F32, BF16 = jnp.float32, jnp.bfloat16


def dot_nn(left, right):
    return jnp.dot(left, right, preferred_element_type=F32)


def dot_tn(left, right):
    return lax.dot_general(left, right, (((0,), (0,)), ((), ())), preferred_element_type=F32)


def dot_nt(left, right):
    return lax.dot_general(left, right, (((1,), (1,)), ((), ())), preferred_element_type=F32)


def deltas(hidden_grad, gate, up):
    sig = jax.nn.sigmoid(gate)
    gate_delta = (hidden_grad * up * sig * (1.0 + gate * (1.0 - sig))).astype(BF16)
    up_delta = (hidden_grad * gate * sig).astype(BF16)
    return gate_delta, up_delta


def activate(gate, up):
    return (gate * jax.nn.sigmoid(gate) * up).astype(BF16)


def make_on_device(mesh):
    n_row, n_col, n_depth = (mesh.shape[a] for a in ("row", "col", "depth"))
    assert n_depth == 4 and n_col == 2 * n_row
    order = [(0, 0), (1, 0), (0, 2), (1, 1), (0, 1), (0, 3), (1, 2), (1, 3)]
    barrier = lax.optimization_barrier

    def swap(x, axis, k):
        n = mesh.shape[axis]
        return lax.ppermute(x, axis, [(i, i ^ k) for i in range(n)])

    def on_device(tokens, cotangent, gate_weight, up_weight, down_weight):
        n, _ = tokens.shape
        feats = gate_weight.shape[0]
        r, d = lax.axis_index("row"), lax.axis_index("depth")

        def by_row(x):
            return [lax.dynamic_index_in_dim(x, r ^ i, 0, keepdims=False) for i in range(n_row)]

        def gather_feats(x):
            pieces = [lax.dynamic_slice(x, (0, 0, (d ^ k) * feats), (2, n, feats)) for k in range(n_depth)]
            pieces = [swap(x, "depth", k) if k else x for k, x in enumerate(pieces)]
            return [[x[i] for x in pieces] for i in range(2)]

        def more_cols(cols, k):
            got = swap(jnp.stack(list(cols.values())), "col", k)
            return {**cols, **{j ^ k: got[i] for i, j in enumerate(cols)}}

        def all_cols(cols, k):
            while k:
                cols = more_cols(cols, k)
                k //= 2
            return cols

        def shares(*parts):
            by_h = [
                jnp.concatenate([parts[k // 2][2 * h + a][k % 2] for a, k in order]) for h in range(n_row)
            ]
            return by_row(jnp.stack(by_h))

        def spread(shares):
            return [shares[0]] + [swap(shares[i], "row", i) for i in range(1, n_row)]

        def tiles(w):
            return [w] + [swap(w, "row", i) for i in range(1, n_row)]

        def part(shares, weights, dot, lo, hi):
            total = dot(shares[0][lo:hi], weights[0])
            for s, w in zip(shares[1:], weights[1:]):
                total = total + dot(s[lo:hi], w)
            return total

        def send_first(sent):
            return swap(sent[: 2 * n], "depth", 1), swap(sent[2 * n :], "depth", 2)

        def second(keep, from_x, from_y):
            a2 = (keep[2 * n : 3 * n] + from_x[n:].astype(F32)).astype(BF16)
            b1 = (keep[3 * n :] + from_y[n:].astype(F32)).astype(BF16)
            return a2, b1

        def total(keep, from_x, from_y, last_y, last_x):
            a0 = keep[:n] + from_x[:n].astype(F32) + last_y.astype(F32)
            b0 = keep[n : 2 * n] + from_y[:n].astype(F32) + last_x.astype(F32)
            return a0, b0

        def gather_row(*blocks):
            x = jnp.concatenate(blocks)
            return [x] + [swap(x, "row", i) for i in range(1, n_row)]

        def cross(b_blocks):
            return swap(b_blocks.astype(BF16), "col", 1).astype(F32)

        def finish(x):
            xs, k = dict(enumerate(by_row(x))), 1
            while k < n_row:
                hs = [h for h in xs if h & k]
                got = swap(jnp.stack([xs.pop(h) for h in hs]).astype(BF16), "col", 2 * k).astype(F32)
                for i, h in enumerate(hs):
                    xs[h ^ k] = xs[h ^ k] + got[i]
                k *= 2
            return xs[0].astype(BF16)

        def direct(a_blocks, b_blocks):
            xs = [x for pair in zip(by_row(a_blocks), by_row(b_blocks)) for x in pair]
            got = [swap(x.astype(BF16), "col", j).astype(F32) for j, x in enumerate(xs) if j]
            return sum(got, xs[0]).astype(BF16)

        def place(*sums):
            outs = jnp.zeros((len(sums), n, feats * n_depth), BF16)
            for k in range(n_depth):
                piece = jnp.stack([x[k] for x in sums])
                piece = swap(piece, "depth", k) if k else piece
                outs = lax.dynamic_update_slice(outs, piece, (0, 0, (d ^ k) * feats))
            return [outs[i] for i in range(len(sums))]

        gws, uws, dws = tiles(gate_weight), tiles(up_weight), tiles(down_weight)
        far, near = n_col // 2, n_col // 4
        tok_own, cot_own = gather_feats(jnp.stack([tokens, cotangent]))
        tok_1, tok_2 = [more_cols({0: jnp.stack(tok_own[i : i + 2])}, far) for i in (0, 2)]
        cot_own, tok_1 = barrier((jnp.stack(cot_own), all_cols(tok_1, near)))
        tok = shares(tok_1, all_cols(tok_2, near))
        tok_shares = spread(tok)
        tok_all = jnp.concatenate(tok).T

        gate_sent = part(tok_shares, gws, dot_nn, 4 * n, 8 * n).astype(BF16)
        gate_got = send_first(gate_sent)
        cot_cols = more_cols({0: cot_own}, far)
        tok_shares, gate_sent = barrier((tok_shares, gate_sent))
        up_sent = part(tok_shares, uws, dot_nn, 4 * n, 8 * n).astype(BF16)
        up_got = send_first(up_sent)
        tok_shares, cot_cols, gate_got, up_sent = barrier((tok_shares, cot_cols, gate_got, up_sent))
        cot_cols = all_cols(cot_cols, near)
        cot = shares({j: x[:2] for j, x in cot_cols.items()}, {j: x[2:] for j, x in cot_cols.items()})
        gate_keep = part(tok_shares, gws, dot_nn, 0, 4 * n)
        a2, b1 = second(gate_keep, *gate_got)
        gate_last = swap(a2, "depth", 2), swap(b1, "depth", 1)
        tok_shares, cot, a2, b1 = barrier((tok_shares, cot, a2, b1))
        up_keep = part(tok_shares, uws, dot_nn, 0, 4 * n)
        cot_shares = spread(cot)
        back_sent = part(cot_shares, dws, dot_nt, 4 * n, 8 * n).astype(BF16)
        back_got = send_first(back_sent)
        up_got, cot_shares, back_sent = barrier((up_got, cot_shares, back_sent))
        a2, b1 = second(up_keep, *up_got)
        up_last = swap(a2, "depth", 2), swap(b1, "depth", 1)
        cot_shares, a2, b1 = barrier((cot_shares, a2, b1))
        back_keep = part(cot_shares, dws, dot_nt, 0, 4 * n)

        gate = total(gate_keep, *gate_got, *gate_last)
        up = total(up_keep, *up_got, *up_last)
        h_a0, h_b0 = [activate(g, u) for g, u in zip(gate, up)]
        h_a2, h_b1 = swap(h_a0, "depth", 2), swap(h_b0, "depth", 1)
        back_got, h_a0, h_b0 = barrier((back_got, h_a0, h_b0))
        a2, b1 = second(back_keep, *back_got)
        back_last = swap(a2, "depth", 2), swap(b1, "depth", 1)
        h_a2, h_b1, a2, b1 = barrier((h_a2, h_b1, a2, b1))
        h_from_x = swap(jnp.concatenate([h_a0, h_a2]), "depth", 1)
        h_from_y = swap(jnp.concatenate([h_b0, h_b1]), "depth", 2)
        hidden_grad = total(back_keep, *back_got, *back_last)
        d_a0, d_b0 = [jnp.concatenate(deltas(h, g, u)) for h, g, u in zip(hidden_grad, gate, up)]
        d_a2, d_b1 = swap(d_a0, "depth", 2), swap(d_b0, "depth", 1)

        def back(rows):
            blocks = rows[0].shape[0] // (2 * n)
            rows = [x.reshape(blocks, 2, n, -1) for x in rows]
            gd, ud = [[x[:, i].reshape(blocks * n, -1) for x in rows] for i in range(2)]
            sums = [dot_nt(g, gate_weight) + dot_nt(u, up_weight) for g, u in zip(gd, ud)]
            return gd, ud, jnp.stack(sums).reshape(n_row, blocks, n, feats)

        gd_e, ud_e, early = back(gather_row(d_a0, d_b0))
        h_from_x, h_from_y, d_a2, d_b1, early = barrier((h_from_x, h_from_y, d_a2, d_b1, early))
        from_x = swap(jnp.concatenate([d_a0, d_a2]), "depth", 1)
        from_y = swap(jnp.concatenate([d_b0, d_b1]), "depth", 2)
        hid_rows = gather_row(h_a0, h_b0, h_a2, h_b1, h_from_x, h_from_y)
        out = jnp.stack([dot_nn(x, down_weight) for x in hid_rows]).reshape(n_row, 8, n, feats)
        middle = gather_row(d_a2, d_b1)
        hid_rows, cot, out, middle = barrier((hid_rows, cot, out, middle))
        done = direct(
            jnp.concatenate([jnp.stack([out[:, i] for i in (0, 4, 2, 5)], axis=1), early[:, :1]], axis=1),
            jnp.concatenate([jnp.stack([out[:, i] for i in (1, 3, 6, 7)], axis=1), early[:, 1:]], axis=1),
        )
        down_grad = dot_tn(jnp.concatenate(hid_rows), jnp.concatenate(cot))
        from_x, from_y, middle, done = barrier((from_x, from_y, middle, done))
        late = [jnp.concatenate(x) for x in zip(middle, gather_row(from_x, from_y))]
        gd_l, ud_l, late = back(late)
        tok_all, late = barrier((tok_all, late))
        got_l = cross(jnp.stack([late[:, i] for i in (1, 4, 5)], axis=1))

        def by_share(e, l):
            return jnp.concatenate([x for pair in zip(e, l) for x in pair])

        gate_grad = dot_nn(tok_all, by_share(gd_e, gd_l))
        tok_all, got_l, gate_grad = barrier((tok_all, got_l, gate_grad))
        rest = finish(jnp.stack([late[:, i] for i in (2, 0, 3)], axis=1) + got_l)
        output, input_grad = place(done[:4], [done[4], *rest])
        up_grad = dot_nn(tok_all, by_share(ud_e, ud_l))
        return output, input_grad, gate_grad, up_grad, down_grad

    return on_device


def solution(mesh):
    act = P(("col", "depth"), "row")
    wide = P(("row", "depth"), "col")
    tall = P("col", ("row", "depth"))
    return jax.shard_map(
        make_on_device(mesh),
        mesh=mesh,
        in_specs=(act, act, wide, wide, tall),
        out_specs=(act, act, wide, wide, tall),
        check_vma=False,
    )
```
